32 devices in a mesh: src: 4 (over y, x), tgt: 8 (over z, core).
Axes of the slice: x: 2, y: 2, z: 4, core: 2. Of those that a mesh axis runs over, the one named last changes fastest.
Arguments:
- pcs_source: bfloat16 [30, 8192], P(None, 'src'), may hold values from -6 to 10
- pcs_target: bfloat16 [30, 16384], P(None, 'tgt'), may hold values from -6 to 6
- growth: float32 [8192], P('src'), may hold values from 0.25 to 4
- scores: bfloat16 [8192, 128], P('src'), may hold values from -6 to 6
Outputs:
- source_potential: float32 [8192], P('src')
- target_potential: float32 [16384], P('tgt')
- transported: float32 [16384, 128], P('tgt')
The draws below stay inside these ranges and needn't reach their ends.
All inputs are finite; a program needn't handle non-finite values.
Results may differ from the reference program's by a relative error of at most 0.0029.
Values sent between devices are 32-bit elements; how exact they have to be, the bound alone decides.
A program may use at most 64 MiB of HBM per device.

```python
import math
import jax
import jax.numpy as jnp
from jax import lax

PCS = 30
PROG = 128
ITERS = 2
NS = 8192
NT = 16384


def draw_pcs_source(key, part):
    base = jnp.clip(jax.random.normal(key, (PCS, NS), jnp.float32), -6.0, 6.0)
    return base.astype(jnp.bfloat16)


def shard_levels(key, dims, cuts, low, top_value):
    def one(dim, shards_of):
        draws = jax.random.uniform(jax.random.fold_in(jax.random.fold_in(key, 6), dim), (shards_of,), jnp.float32, low / len(cuts), top_value / len(cuts))
        return jnp.repeat(jnp.exp(draws), dims[dim] // shards_of).reshape((-1,) + (1,) * (len(dims) - dim - 1))

    level = one(*cuts[0])
    for cut in cuts[1:]:
        level = level * one(*cut)
    return level


def scatter_about(key, dims, deviation, limit, cuts=(), held_as=jnp.bfloat16):
    values = jax.random.normal(key, dims, jnp.float32) * deviation
    if len(cuts) > 0:
        values = shard_levels(key, dims, cuts, -0.22, 0.18) * values
    return jnp.clip(values, min=-limit, max=limit).astype(held_as)


def setup_inputs(seed: int = 0) -> dict:
    arg_keys = jax.random.split(jax.random.key(seed), 5)
    return {
        "pcs_source": draw_pcs_source(jax.random.fold_in(arg_keys[4], 71), 0),
        "pcs_target": scatter_about(arg_keys[1], (PCS, NT), 1.0, 6.0, ((1, 8),)),
        "growth": jnp.clip(jnp.exp(math.log(4.0) - 2.7725887 * jax.random.uniform(arg_keys[2], (NS,), jnp.float32) ** shard_levels(arg_keys[2], (NS,), ((0, 4),), -0.2, 0.2)), 0.25, 4.0),
        "scores": scatter_about(arg_keys[3], (NS, PROG), 1.0, 6.0, ((0, 4),)),
    }


EPSILON = 0.05
MARGIN = 1.0
FACTOR = MARGIN / (MARGIN + EPSILON)


def cost_tile(left, right):
    cross = lax.dot_general(left, right, (((0,), (0,)), ((), ())), preferred_element_type=jnp.float32)
    left_wide = left.astype(jnp.float32)
    right_wide = right.astype(jnp.float32)
    left_sq = jnp.sum(left_wide * left_wide, axis=0)
    right_sq = jnp.sum(right_wide * right_wide, axis=0)
    return (left_sq[:, None] + right_sq[None, :] - 2.0 * cross) / left.shape[0]


def stacked(coords, width):
    return jnp.transpose(coords.reshape(coords.shape[0], -1, width), (1, 0, 2))


def log_sum_rows(logits):
    peak = jnp.max(logits, axis=1)
    return peak + jnp.log(jnp.sum(jnp.exp(logits - peak[:, None]), axis=1))


def reference(pcs_source, pcs_target, growth, scores):
    total_sources = pcs_source.shape[1]
    total_targets = pcs_target.shape[1]
    source_width = math.gcd(total_sources, 256)
    target_width = math.gcd(total_targets, 256)
    source_blocks = stacked(pcs_source, source_width)
    target_blocks = stacked(pcs_target, target_width)
    log_a = jnp.log(growth) - jnp.log(jnp.float32(total_sources))
    log_b = -jnp.log(jnp.float32(total_targets))
    source_potential = jnp.zeros((total_sources,), jnp.float32)
    target_potential = jnp.zeros((total_targets,), jnp.float32)
    for step in range(ITERS):
        gpot = target_potential
        rows = lax.map(lambda block: log_sum_rows((gpot[None, :] - cost_tile(block, pcs_target)) / EPSILON), source_blocks).reshape(-1)
        source_potential = FACTOR * (EPSILON * log_a - EPSILON * rows)
        fpot = source_potential
        columns = lax.map(lambda block: log_sum_rows((fpot[None, :] - cost_tile(block, pcs_source)) / EPSILON), target_blocks).reshape(-1)
        target_potential = FACTOR * (EPSILON * log_b - EPSILON * columns)

    def carry_block(pair):
        block, gblock = pair
        tile = cost_tile(block, pcs_source)
        plan = jnp.exp((source_potential[None, :] + gblock[:, None] - tile) / EPSILON)
        mass = jnp.sum(plan, axis=1)
        carried = jnp.dot(plan.astype(jnp.bfloat16), scores, preferred_element_type=jnp.float32)
        return carried / mass[:, None]

    transported = lax.map(carry_block, (target_blocks, target_potential.reshape(-1, target_width))).reshape(total_targets, -1)
    return source_potential, target_potential, transported
```

```python
import functools
import math

import jax
import jax.numpy as jnp
from jax import lax
from jax.experimental import pallas as pl
from jax.experimental.pallas import tpu as pltpu
from jax.sharding import PartitionSpec as P

ITERS = 2
EPSILON = 0.05
MARGIN = 1.0
FACTOR = MARGIN / (MARGIN + EPSILON)
LANES = 128
LOG2E = math.log2(math.e)
UNIT = EPSILON / LOG2E
MESH = pl.DeviceIdType.MESH


def augment(coords_ref, wide_ref, rows_ref, columns_ref, norm_first):
    pcs, cells = coords_ref.shape
    wide = coords_ref[...].astype(jnp.float32)
    norm = -0.5 * jnp.sum(wide * wide, axis=0, keepdims=True)
    high = norm.astype(jnp.bfloat16).astype(jnp.float32)
    mid = (norm - high).astype(jnp.bfloat16).astype(jnp.float32)
    low = norm - high - mid
    base = -(-pcs // 8) * 8
    at = lax.broadcasted_iota(jnp.int32, (8, cells), 0) - (0 if norm_first else 3)
    one = jnp.where((at >= 3) & (at < 6) if norm_first else (at < 0), 1.0, 0.0)
    extra = jnp.where(at == 0, high, jnp.where(at == 1, mid, jnp.where(at == 2, low, one)))
    wide_ref[...] = jnp.zeros(wide_ref.shape, jnp.float32)
    wide_ref[0:pcs, :] = wide
    wide_ref[base : base + 8, :] = extra
    for k in range(cells // LANES):
        cut = slice(k * LANES, (k + 1) * LANES)
        piece = wide_ref[:, cut]
        rows_ref[cut, :] = piece.T.astype(jnp.bfloat16)
        columns_ref[:, cut] = piece.astype(jnp.bfloat16)


def spread(dense, out_ref):
    for k in range(dense.shape[0]):
        out_ref[k * LANES : (k + 1) * LANES, :] = jnp.broadcast_to(
            dense[k : k + 1, :], (LANES, LANES)
        ).T


def join(peak, total, block):
    t = block.reshape(-1, 8, LANES)
    newpeak = jnp.maximum(peak, jnp.max(t, axis=0))
    total = total * jnp.exp2(peak - newpeak) + jnp.sum(jnp.exp2(t - newpeak[None]), axis=0)
    return newpeak, total


def closed(peak, total):
    top = jnp.max(peak, axis=0, keepdims=True)
    return top, jnp.sum(total * jnp.exp2(peak - top), axis=0, keepdims=True)


def column_pass(tile_ref, bias_ref, lse_ref, make=None):
    rows, columns = tile_ref.shape
    width = math.gcd(columns, 256)
    step = math.gcd(rows, 256)
    sub = math.gcd(step, 128)
    halves = width // LANES

    def over_columns(c, unused):
        start = pl.multiple_of(c * width, width)

        def over_rows(r, carry):
            row = pl.multiple_of(r * step, step)
            if make is not None:
                tile_ref[pl.ds(row, step), pl.ds(start, width)] = make(
                    pl.ds(row, step), pl.ds(start, width)
                )
            carry = list(carry)
            for q in range(step // sub):
                at = pl.ds(pl.multiple_of(row + q * sub, sub), sub)
                for h in range(halves):
                    lanes = pl.ds(pl.multiple_of(start + h * LANES, LANES), LANES)
                    block = tile_ref[at, lanes]
                    if bias_ref is not None:
                        block = block + bias_ref[at, :]
                    carry[h] = join(*carry[h], block)
            return tuple(carry)

        empty = (jnp.full((8, LANES), -jnp.inf, jnp.float32), jnp.zeros((8, LANES), jnp.float32))
        stats = lax.fori_loop(0, rows // step, over_rows, (empty,) * halves)
        for h in range(halves):
            top, total = closed(*stats[h])
            lse_ref[pl.ds(c * halves + h, 1), :] = top + jnp.log2(total)
        return unused

    lax.fori_loop(0, columns // width, over_columns, 0)


def kernel(
    n_src, n_tgt, xs_ref, yt_ref, growth_ref, scores_ref, f_ref, g_ref, out_ref,
    tile, tile_t, wide, x_rows, x_cols, y_rows, y_cols, scores_t, bias, weights, carried, partial,
    lse, row_buf, col_buf, stat, received, row_send, row_recv, col_send, col_recv,
    stat_send, stat_recv, part_send, part_recv, out_send, out_recv,
):
    src, tgt = lax.axis_index("src"), lax.axis_index("tgt")
    barrier = pltpu.get_barrier_semaphore()
    for k in range(1, n_src):
        pl.semaphore_signal(
            barrier, inc=1, device_id={"src": lax.rem(src + k, n_src)}, device_id_type=MESH
        )
    for k in range(1, n_tgt):
        pl.semaphore_signal(
            barrier, inc=1, device_id={"tgt": lax.rem(tgt + k, n_tgt)}, device_id_type=MESH
        )

    rows, columns = tile.shape
    scale = 2.0 * LOG2E / (xs_ref.shape[0] * EPSILON)
    augment(xs_ref, wide.at[:, 0:rows], x_rows, x_cols, False)
    augment(yt_ref, wide.at[:, 0:columns], y_rows, y_cols, True)

    def filled(left, right):
        def make(at, lanes):
            return scale * lax.dot_general(
                left[at, :], right[:, lanes], (((1,), (0,)), ((), ())),
                preferred_element_type=jnp.float32,
            )
        return make

    def exchange(buf, axis, me, n, send, recv):
        copies = [
            pltpu.make_async_remote_copy(
                src_ref=buf.at[me], dst_ref=buf.at[me], send_sem=send.at[k], recv_sem=recv.at[k],
                device_id={axis: lax.rem(me + k, n)}, device_id_type=MESH,
            )
            for k in range(1, n)
        ]
        for copy in copies:
            copy.start()
        return copies

    def joined(buf, n):
        parts = [buf[d] for d in range(n)]
        top = functools.reduce(jnp.maximum, parts)
        return top + jnp.log2(sum(jnp.exp2(part - top) for part in parts))

    log_a = jnp.log2(growth_ref[...]) - math.log2(rows * n_src)
    log_b = -math.log2(columns * n_tgt)
    for step in range(ITERS):
        first = step == 0
        column_pass(
            tile_t, None if first else bias.at[0:columns, :], row_buf.at[step, tgt],
            filled(y_rows, x_cols) if first else None,
        )
        if first:
            pl.semaphore_wait(barrier, n_src + n_tgt - 2)
        copies = exchange(row_buf.at[step], "tgt", tgt, n_tgt, row_send.at[step], row_recv.at[step])
        if first:
            for k in range(rows // LANES):
                cut = slice(k * LANES, (k + 1) * LANES)
                scores_t[:, cut] = scores_ref[cut, :].astype(jnp.float32).T.astype(jnp.bfloat16)
        for copy in copies:
            copy.wait()
        potential = FACTOR * (log_a - joined(row_buf.at[step], n_tgt))
        spread(potential, bias)
        if step < ITERS - 1:
            column_pass(
                tile, bias.at[0:rows, :], col_buf.at[step, src],
                filled(x_rows, y_cols) if first else None,
            )
            copies = exchange(
                col_buf.at[step], "src", src, n_src, col_send.at[step], col_recv.at[step]
            )
            for copy in copies:
                copy.wait()
            spread(FACTOR * (log_b - joined(col_buf.at[step], n_src)), bias)
    f_ref[...] = UNIT * potential

    piece = columns // n_src
    width = math.gcd(piece, 256)
    depth = math.gcd(rows, 256)
    halves = width // LANES
    sub = math.gcd(depth, 128)
    parts = []
    for k in range(1, n_src + 1):
        owner = lax.rem(src + k, n_src)

        def over_tiles(c, unused, owner=owner):
            start = pl.multiple_of(owner * piece + c * width, width)

            def tops(r, peaks):
                at = pl.ds(pl.multiple_of(r * depth, depth), depth)
                peaks = list(peaks)
                for h in range(halves):
                    lanes = pl.ds(pl.multiple_of(start + h * LANES, LANES), LANES)
                    block = tile[at, lanes] + bias[at, :]
                    peaks[h] = jnp.maximum(peaks[h], jnp.max(block.reshape(-1, 8, LANES), axis=0))
                return tuple(peaks)

            peaks = lax.fori_loop(
                0, rows // depth, tops,
                (jnp.full((8, LANES), -jnp.inf, jnp.float32),) * halves,
            )
            peaks = [jnp.max(peak, axis=0, keepdims=True) for peak in peaks]

            def plan(r, totals):
                row = pl.multiple_of(r * depth, depth)
                totals = list(totals)
                for q in range(depth // sub):
                    at = pl.ds(pl.multiple_of(row + q * sub, sub), sub)
                    for h in range(halves):
                        lanes = pl.ds(pl.multiple_of(start + h * LANES, LANES), LANES)
                        w = jnp.exp2(tile[at, lanes] + bias[at, :] - peaks[h])
                        totals[h] = totals[h] + jnp.sum(w.reshape(-1, 8, LANES), axis=0)
                        weights[at, h * LANES : (h + 1) * LANES] = w.astype(jnp.bfloat16)
                return tuple(totals)

            totals = lax.fori_loop(
                0, rows // depth, plan, (jnp.zeros((8, LANES), jnp.float32),) * halves
            )
            carried[...] = jnp.dot(scores_t[...], weights[...], preferred_element_type=jnp.float32)
            for h in range(halves):
                stat[src, 0, pl.ds(start // LANES + h, 1), :] = jnp.sum(
                    totals[h], axis=0, keepdims=True
                )
                stat[src, 1, pl.ds(start // LANES + h, 1), :] = peaks[h]
                at = pl.ds(pl.multiple_of(start + h * LANES, LANES), LANES)
                partial[at, :] = carried[:, h * LANES : (h + 1) * LANES].T
            return unused

        lax.fori_loop(0, piece // width, over_tiles, 0)
        if k < n_src:
            copy = pltpu.make_async_remote_copy(
                src_ref=partial.at[pl.ds(pl.multiple_of(owner * piece, piece), piece), :],
                dst_ref=received.at[k], send_sem=part_send.at[k], recv_sem=part_recv.at[k],
                device_id={"src": owner}, device_id_type=MESH,
            )
            copy.start()
            parts.append(copy)
    copies = exchange(stat, "src", src, n_src, stat_send, stat_recv)
    for copy in copies:
        copy.wait()
    peak = functools.reduce(jnp.maximum, [stat[d, 1] for d in range(n_src)])
    total = sum(stat[d, 0] * jnp.exp2(stat[d, 1] - peak) for d in range(n_src))
    g_ref[...] = UNIT * FACTOR * (log_b - (peak + jnp.log2(total)))
    for d in range(n_src):
        stat[d, 0] = jnp.exp2(stat[d, 1] - peak) / total
    for copy in parts:
        copy.wait()
    first_row = src * (piece // LANES)
    for q in range(piece // LANES):
        mine = pl.ds(pl.multiple_of(src * piece + q * LANES, LANES), LANES)
        result = None
        for k in range(n_src):
            sender = lax.rem(src - k + n_src, n_src)
            share = jnp.broadcast_to(
                stat[sender, 0, pl.ds(first_row + q, 1), :], (LANES, LANES)
            ).T
            block = partial[mine, :] if k == 0 else received[k, q * LANES : (q + 1) * LANES, :]
            result = share * block if result is None else result + share * block
        out_ref[mine, :] = result
    mine = pl.ds(pl.multiple_of(src * piece, piece), piece)
    copies = [
        pltpu.make_async_remote_copy(
            src_ref=out_ref.at[mine, :], dst_ref=out_ref.at[mine, :],
            send_sem=out_send.at[k], recv_sem=out_recv.at[k],
            device_id={"src": lax.rem(src + k, n_src)}, device_id_type=MESH,
        )
        for k in range(1, n_src)
    ]
    for copy in copies:
        copy.start()
    for copy in copies:
        copy.wait()


def solution(mesh):
    n_src, n_tgt = mesh.shape["src"], mesh.shape["tgt"]

    def shards(pcs_source, pcs_target, growth, scores):
        rows, columns = pcs_source.shape[1], pcs_target.shape[1]
        programs = scores.shape[1]
        piece = columns // n_src
        f32, bf16 = jnp.float32, jnp.bfloat16
        sem = pltpu.SemaphoreType.DMA
        whole = pl.BlockSpec(memory_space=pltpu.VMEM)
        dense_r, dense_c = (rows // LANES, LANES), (columns // LANES, LANES)
        f, g, out = pl.pallas_call(
            functools.partial(kernel, n_src, n_tgt),
            out_shape=(
                jax.ShapeDtypeStruct(dense_r, f32),
                jax.ShapeDtypeStruct(dense_c, f32),
                jax.ShapeDtypeStruct((columns, programs), f32),
            ),
            in_specs=[whole] * 4,
            out_specs=(whole,) * 3,
            scratch_shapes=[
                pltpu.VMEM((rows, columns), f32),
                pltpu.VMEM((columns, rows), f32),
                pltpu.VMEM((LANES, max(rows, columns)), f32),
                pltpu.VMEM((rows, LANES), bf16),
                pltpu.VMEM((LANES, rows), bf16),
                pltpu.VMEM((columns, LANES), bf16),
                pltpu.VMEM((LANES, columns), bf16),
                pltpu.VMEM((programs, rows), bf16),
                pltpu.VMEM((max(rows, columns), LANES), f32),
                pltpu.VMEM((rows, math.gcd(piece, 256)), bf16),
                pltpu.VMEM((programs, math.gcd(piece, 256)), f32),
                pltpu.VMEM((columns, programs), f32),
                pltpu.VMEM((8, LANES), f32),
                pltpu.VMEM((ITERS, n_tgt) + dense_r, f32),
                pltpu.VMEM((ITERS, n_src) + dense_c, f32),
                pltpu.VMEM((n_src, 2) + dense_c, f32),
                pltpu.VMEM((n_src, piece, programs), f32),
                sem((ITERS, n_tgt)),
                sem((ITERS, n_tgt)),
                sem((ITERS, n_src)),
                sem((ITERS, n_src)),
                sem((n_src,)),
                sem((n_src,)),
                sem((n_src,)),
                sem((n_src,)),
                sem((n_src,)),
                sem((n_src,)),
            ],
            compiler_params=pltpu.CompilerParams(
                collective_id=0, has_side_effects=True, vmem_limit_bytes=60 * 2**20
            ),
            name="coupling",
        )(pcs_source, pcs_target, growth.reshape(dense_r), scores)
        return f.reshape(-1), g.reshape(-1), out

    in_specs = (P(None, "src"), P(None, "tgt"), P("src"), P("src", None))
    out_specs = (P("src"), P("tgt"), P("tgt", None))
    return jax.shard_map(shards, mesh=mesh, in_specs=in_specs, out_specs=out_specs, check_vma=False)
```

```python
import functools
import math

import jax
import jax.numpy as jnp
from jax import lax
from jax.experimental import pallas as pl
from jax.experimental.pallas import tpu as pltpu
from jax.sharding import PartitionSpec as P

ITERS = 2
EPSILON = 0.05
MARGIN = 1.0
FACTOR = MARGIN / (MARGIN + EPSILON)
LANES = 128
LOG2E = math.log2(math.e)
UNIT = EPSILON / LOG2E
MESH = pl.DeviceIdType.MESH
WIDTH, STEP, SUB = 512, 256, 64
DEPTH = 2048


def augment(coords_ref, wide_ref, rows_ref, columns_ref, norm_first):
    pcs, cells = coords_ref.shape
    wide = coords_ref[...].astype(jnp.float32)
    norm = -0.5 * jnp.sum(wide * wide, axis=0, keepdims=True)
    high = norm.astype(jnp.bfloat16).astype(jnp.float32)
    mid = (norm - high).astype(jnp.bfloat16).astype(jnp.float32)
    low = norm - high - mid
    base = -(-pcs // 8) * 8
    at = lax.broadcasted_iota(jnp.int32, (8, cells), 0) - (0 if norm_first else 3)
    one = jnp.where((at >= 3) & (at < 6) if norm_first else (at < 0), 1.0, 0.0)
    extra = jnp.where(at == 0, high, jnp.where(at == 1, mid, jnp.where(at == 2, low, one)))
    wide_ref[...] = jnp.zeros(wide_ref.shape, jnp.float32)
    wide_ref[0:pcs, :] = wide
    wide_ref[base : base + 8, :] = extra
    for k in range(cells // LANES):
        cut = slice(k * LANES, (k + 1) * LANES)
        piece = wide_ref[:, cut]
        rows_ref[cut, :] = piece.T.astype(jnp.bfloat16)
        columns_ref[:, cut] = piece.astype(jnp.bfloat16)


def spread(dense, out_ref):
    for k in range(dense.shape[0]):
        out_ref[k * LANES : (k + 1) * LANES, :] = jnp.broadcast_to(
            dense[k : k + 1, :], (LANES, LANES)
        ).T


def join(peak, total, block):
    t = block.reshape(-1, 8, LANES)
    newpeak = jnp.maximum(peak, jnp.max(t, axis=0))
    total = total * jnp.exp2(peak - newpeak) + jnp.sum(jnp.exp2(t - newpeak[None]), axis=0)
    return newpeak, total


def closed(peak, total):
    top = jnp.max(peak, axis=0, keepdims=True)
    return top, jnp.sum(total * jnp.exp2(peak - top), axis=0, keepdims=True)


def column_pass(tile_ref, bias_ref, lse_ref, make=None):
    rows, columns = tile_ref.shape
    width = math.gcd(columns, WIDTH)
    step = math.gcd(rows, STEP)
    sub = math.gcd(step, SUB)
    halves = width // LANES

    def over_columns(c, unused):
        start = pl.multiple_of(c * width, width)
        lanes = [pl.ds(pl.multiple_of(start + h * LANES, LANES), LANES) for h in range(halves)]

        def fill(r):
            at = pl.ds(r * step, step)
            tile_ref[at, pl.ds(start, width)] = make(at, pl.ds(start, width))

        empty = (jnp.full((8, LANES), -jnp.inf, jnp.float32), jnp.zeros((8, LANES), jnp.float32))
        stats = [empty] * halves
        if make is not None:
            fill(0)
        for r in range(rows // step):
            if make is not None and r + 1 < rows // step:
                fill(r + 1)
            for q in range(step // sub):
                at = pl.ds(r * step + q * sub, sub)
                for h in range(halves):
                    block = tile_ref[at, lanes[h]]
                    if bias_ref is not None:
                        block = block + bias_ref[at, :]
                    stats[h] = join(*stats[h], block)
        for h in range(halves):
            top, total = closed(*stats[h])
            lse_ref[pl.ds(c * halves + h, 1), :] = top + jnp.log2(total)
        return unused

    lax.fori_loop(0, columns // width, over_columns, 0)


def carry_tile(tile_ref, bias_ref, scores_ref, weights, start, width):
    rows = tile_ref.shape[0]
    halves = width // LANES
    sub = math.gcd(rows, SUB)
    step = math.gcd(rows, DEPTH)
    lanes = [pl.ds(pl.multiple_of(start + h * LANES, LANES), LANES) for h in range(halves)]
    peaks = [jnp.full((8, LANES), -jnp.inf, jnp.float32)] * halves
    for r in range(rows // sub):
        at = pl.ds(r * sub, sub)
        for h in range(halves):
            block = tile_ref[at, lanes[h]] + bias_ref[at, :]
            peaks[h] = jnp.maximum(peaks[h], jnp.max(block.reshape(-1, 8, LANES), axis=0))
    peaks = [jnp.max(peak, axis=0, keepdims=True) for peak in peaks]
    totals = [jnp.zeros((8, LANES), jnp.float32)] * halves
    for r in range(rows // sub):
        at = pl.ds(r * sub, sub)
        for h in range(halves):
            w = jnp.exp2(tile_ref[at, lanes[h]] + bias_ref[at, :] - peaks[h])
            totals[h] = totals[h] + jnp.sum(w.reshape(-1, 8, LANES), axis=0)
            weights[at, h * LANES : (h + 1) * LANES] = w.astype(jnp.bfloat16)
    carried = None
    for r in range(rows // step):
        at = slice(r * step, (r + 1) * step)
        part = jnp.dot(scores_ref[:, at], weights[at, 0:width], preferred_element_type=jnp.float32)
        carried = part if carried is None else carried + part
    return peaks, [jnp.sum(total, axis=0, keepdims=True) for total in totals], carried


def kernel(
    n_src, n_tgt, xs_ref, yt_ref, growth_ref, scores_ref, f_ref, g_ref, out_ref,
    tile, tile_t, wide, x_rows, x_cols, y_rows, y_cols, scores_t, bias, weights, partial,
    row_buf, col_buf, stat, received, row_send, row_recv, col_send, col_recv,
    stat_send, stat_recv, part_send, part_recv, out_send, out_recv,
):
    src, tgt = lax.axis_index("src"), lax.axis_index("tgt")
    barrier = pltpu.get_barrier_semaphore()
    for k in range(1, n_src):
        pl.semaphore_signal(
            barrier, inc=1, device_id={"src": lax.rem(src + k, n_src)}, device_id_type=MESH
        )
    for k in range(1, n_tgt):
        pl.semaphore_signal(
            barrier, inc=1, device_id={"tgt": lax.rem(tgt + k, n_tgt)}, device_id_type=MESH
        )

    rows, columns = tile.shape
    scale = 2.0 * LOG2E / (xs_ref.shape[0] * EPSILON)
    augment(xs_ref, wide.at[:, 0:rows], x_rows, x_cols, False)
    augment(yt_ref, wide.at[:, 0:columns], y_rows, y_cols, True)

    def filled(left, right):
        def make(at, lanes):
            return scale * lax.dot_general(
                left[at, :], right[:, lanes], (((1,), (0,)), ((), ())),
                preferred_element_type=jnp.float32,
            )
        return make

    def exchange(buf, axis, me, n, send, recv):
        copies = [
            pltpu.make_async_remote_copy(
                src_ref=buf.at[me], dst_ref=buf.at[me], send_sem=send.at[k], recv_sem=recv.at[k],
                device_id={axis: lax.rem(me + k, n)}, device_id_type=MESH,
            )
            for k in range(1, n)
        ]
        for copy in copies:
            copy.start()
        return copies

    def joined(buf, n):
        parts = [buf[d] for d in range(n)]
        top = functools.reduce(jnp.maximum, parts)
        return top + jnp.log2(sum(jnp.exp2(part - top) for part in parts))

    log_a = jnp.log2(growth_ref[...]) - math.log2(rows * n_src)
    log_b = -math.log2(columns * n_tgt)
    for step in range(ITERS):
        first = step == 0
        column_pass(
            tile_t, None if first else bias.at[0:columns, :], row_buf.at[step, tgt],
            filled(y_rows, x_cols) if first else None,
        )
        if first:
            pl.semaphore_wait(barrier, n_src + n_tgt - 2)
        copies = exchange(row_buf.at[step], "tgt", tgt, n_tgt, row_send.at[step], row_recv.at[step])
        if first:
            for k in range(rows // LANES):
                cut = slice(k * LANES, (k + 1) * LANES)
                scores_t[:, cut] = scores_ref[cut, :].astype(jnp.float32).T.astype(jnp.bfloat16)
        for copy in copies:
            copy.wait()
        potential = FACTOR * (log_a - joined(row_buf.at[step], n_tgt))
        spread(potential, bias)
        if step < ITERS - 1:
            column_pass(
                tile, bias.at[0:rows, :], col_buf.at[step, src],
                filled(x_rows, y_cols) if first else None,
            )
            copies = exchange(
                col_buf.at[step], "src", src, n_src, col_send.at[step], col_recv.at[step]
            )
            for copy in copies:
                copy.wait()
            spread(FACTOR * (log_b - joined(col_buf.at[step], n_src)), bias)
    f_ref[...] = UNIT * potential

    piece = columns // n_src
    width = math.gcd(piece, WIDTH)
    halves = width // LANES
    parts = []
    for k in range(1, n_src + 1):
        owner = lax.rem(src + k, n_src)

        def over_tiles(c, unused, owner=owner):
            start = pl.multiple_of(owner * piece + c * width, width)
            peaks, totals, carried = carry_tile(tile, bias, scores_t, weights, start, width)
            for h in range(halves):
                stat[src, 0, pl.ds(start // LANES + h, 1), :] = totals[h]
                stat[src, 1, pl.ds(start // LANES + h, 1), :] = peaks[h]
                at = pl.ds(pl.multiple_of(start + h * LANES, LANES), LANES)
                partial[at, :] = carried[:, h * LANES : (h + 1) * LANES].T
            return unused

        lax.fori_loop(0, piece // width, over_tiles, 0)
        if k < n_src:
            copy = pltpu.make_async_remote_copy(
                src_ref=partial.at[pl.ds(pl.multiple_of(owner * piece, piece), piece), :],
                dst_ref=received.at[k], send_sem=part_send.at[k], recv_sem=part_recv.at[k],
                device_id={"src": owner}, device_id_type=MESH,
            )
            copy.start()
            parts.append(copy)
    copies = exchange(stat, "src", src, n_src, stat_send, stat_recv)
    for copy in copies:
        copy.wait()
    peak = functools.reduce(jnp.maximum, [stat[d, 1] for d in range(n_src)])
    total = sum(stat[d, 0] * jnp.exp2(stat[d, 1] - peak) for d in range(n_src))
    g_ref[...] = UNIT * FACTOR * (log_b - (peak + jnp.log2(total)))
    for d in range(n_src):
        stat[d, 0] = jnp.exp2(stat[d, 1] - peak) / total
    for copy in parts:
        copy.wait()
    first_row = src * (piece // LANES)
    for q in range(piece // LANES):
        mine = pl.ds(pl.multiple_of(src * piece + q * LANES, LANES), LANES)
        result = None
        for k in range(n_src):
            sender = lax.rem(src - k + n_src, n_src)
            share = jnp.broadcast_to(
                stat[sender, 0, pl.ds(first_row + q, 1), :], (LANES, LANES)
            ).T
            block = partial[mine, :] if k == 0 else received[k, q * LANES : (q + 1) * LANES, :]
            result = share * block if result is None else result + share * block
        out_ref[mine, :] = result
    mine = pl.ds(pl.multiple_of(src * piece, piece), piece)
    copies = [
        pltpu.make_async_remote_copy(
            src_ref=out_ref.at[mine, :], dst_ref=out_ref.at[mine, :],
            send_sem=out_send.at[k], recv_sem=out_recv.at[k],
            device_id={"src": lax.rem(src + k, n_src)}, device_id_type=MESH,
        )
        for k in range(1, n_src)
    ]
    for copy in copies:
        copy.start()
    for copy in copies:
        copy.wait()


def solution(mesh):
    n_src, n_tgt = mesh.shape["src"], mesh.shape["tgt"]

    def shards(pcs_source, pcs_target, growth, scores):
        rows, columns = pcs_source.shape[1], pcs_target.shape[1]
        programs = scores.shape[1]
        piece = columns // n_src
        f32, bf16 = jnp.float32, jnp.bfloat16
        sem = pltpu.SemaphoreType.DMA
        whole = pl.BlockSpec(memory_space=pltpu.VMEM)
        dense_r, dense_c = (rows // LANES, LANES), (columns // LANES, LANES)
        f, g, out = pl.pallas_call(
            functools.partial(kernel, n_src, n_tgt),
            out_shape=(
                jax.ShapeDtypeStruct(dense_r, f32),
                jax.ShapeDtypeStruct(dense_c, f32),
                jax.ShapeDtypeStruct((columns, programs), f32),
            ),
            in_specs=[whole] * 4,
            out_specs=(whole,) * 3,
            scratch_shapes=[
                pltpu.VMEM((rows, columns), f32),
                pltpu.VMEM((columns, rows), f32),
                pltpu.VMEM((LANES, max(rows, columns)), f32),
                pltpu.VMEM((rows, LANES), bf16),
                pltpu.VMEM((LANES, rows), bf16),
                pltpu.VMEM((columns, LANES), bf16),
                pltpu.VMEM((LANES, columns), bf16),
                pltpu.VMEM((programs, rows), bf16),
                pltpu.VMEM((max(rows, columns), LANES), f32),
                pltpu.VMEM((rows, math.gcd(piece, WIDTH)), bf16),
                pltpu.VMEM((columns, programs), f32),
                pltpu.VMEM((ITERS, n_tgt) + dense_r, f32),
                pltpu.VMEM((ITERS, n_src) + dense_c, f32),
                pltpu.VMEM((n_src, 2) + dense_c, f32),
                pltpu.VMEM((n_src, piece, programs), f32),
                sem((ITERS, n_tgt)),
                sem((ITERS, n_tgt)),
                sem((ITERS, n_src)),
                sem((ITERS, n_src)),
                sem((n_src,)),
                sem((n_src,)),
                sem((n_src,)),
                sem((n_src,)),
                sem((n_src,)),
                sem((n_src,)),
            ],
            compiler_params=pltpu.CompilerParams(
                collective_id=0, has_side_effects=True, vmem_limit_bytes=60 * 2**20
            ),
            name="coupling",
        )(pcs_source, pcs_target, growth.reshape(dense_r), scores)
        return f.reshape(-1), g.reshape(-1), out

    in_specs = (P(None, "src"), P(None, "tgt"), P("src"), P("src", None))
    out_specs = (P("src"), P("tgt"), P("tgt", None))
    return jax.shard_map(shards, mesh=mesh, in_specs=in_specs, out_specs=out_specs, check_vma=False)
```
